32 devices in a mesh: dom: 32 (over z, y, x, core).
Axes of the slice: x: 2, y: 2, z: 4, core: 2. Of those that a mesh axis runs over, the one named last changes fastest.
Arguments:
- features: bfloat16 [16384, 512], P('dom'), may hold values from -6 to 6
- weight: bfloat16 [512, 512], replicated, may hold values from -0.25 to 0.25
- grad_out: bfloat16 [16384, 512], P('dom'), may hold values from -6 to 6
- adjacency: bfloat16 [768, 128, 128], P('dom'), may hold values from -0.25 to 0.25
- tile_row: int32 [32, 24], P('dom'), may hold values from 0 to 3
- tile_src: int32 [32, 24], P('dom'), may hold values from 0 to 7
- tile_count: int32 [32], P('dom'), may hold values from 1 to 24, as said below
- send_tile: int32 [32, 4], P('dom'), may hold values from 0 to 3
- stale_feat: bfloat16 [32, 4, 128, 512], P('dom'), may hold values from -6 to 6
- stale_grad: bfloat16 [32, 4, 128, 512], P('dom'), may hold values from -6 to 6
- blend: float32 [512], replicated, may hold values from 0.2 to 0.8
Outputs:
- output: bfloat16 [16384, 512], P('dom')
- grad_features: bfloat16 [16384, 512], P('dom')
- grad_weight: bfloat16 [512, 512], replicated
The draws below stay inside these ranges and needn't reach their ends.
Inputs may be any that keep to these rules, and one draw needn't show every extreme that they name: `tile_count`: counts are skewed; some partition holds all 24 entries.
All inputs are finite; a program needn't handle non-finite values.
Results may differ from the reference program's by a relative error of at most 0.0064.
Values may be sent and summed in bfloat16 or wider, within the bound.
A program may use at most 64 MiB of HBM per device.

```python
import jax
import jax.numpy as jnp
from jax import lax

WIDTH = 512
BLOCK = 128
NODES_DEV = 512
TILE_ENT = 24
ROUNDS = 4
TILES_DEV = 4
NODES = 16384
ENTRIES = 768
N_DOM = 32


def draw_tile_count(key, part):
    first_key, second_key = jax.random.split(jax.random.fold_in(key, 17))
    levels = jax.random.randint(first_key, (N_DOM,), 0, 8)
    counts = jnp.maximum(TILE_ENT // (1 + levels), 1)
    chosen = jax.random.randint(second_key, (), 0, N_DOM)
    return counts.at[chosen].set(TILE_ENT).astype(jnp.int32)


def set_ends(array, own_key, low, top_value):
    shape = array.shape
    index_at = [jax.random.randint(jax.random.fold_in(own_key, axis), (), 0, shape[axis]) for axis in range(len(shape))]
    array = array.at[tuple(index_at)].set(low)
    longest = shape.index(max(shape))
    index_at[longest] = (index_at[longest] + 1) % shape[longest]
    return array.at[tuple(index_at)].set(top_value)


def block_scale(rng, extent, cuts, smallest, largest):
    def one(position, parts):
        heights = jax.random.uniform(jax.random.fold_in(jax.random.fold_in(rng, 6), position), (parts,), jnp.float32, smallest / len(cuts), largest / len(cuts))
        return jnp.repeat(jnp.exp(heights), extent[position] // parts).reshape((-1,) + (1,) * (len(extent) - position - 1))

    gain = one(*cuts[0])
    for cut in cuts[1:]:
        gain = gain * one(*cut)
    return gain


def gaussian(rng, dims, width, bound, pieces=(), kind=jnp.bfloat16):
    result = jax.random.normal(rng, dims, jnp.float32) * width
    if len(pieces) > 0:
        result = block_scale(rng, dims, pieces, -0.22, 0.18) * result
    return jnp.clip(result, min=-bound, max=bound).astype(kind)


def setup_inputs(seed: int = 0) -> dict:
    keys = jax.random.split(jax.random.key(seed), 12)
    features = gaussian(keys[0], (NODES, WIDTH), 1.0, 6.0, ((0, 32),))
    weight = gaussian(keys[1], (WIDTH, WIDTH), WIDTH ** -0.5, 0.25)
    grad_out = gaussian(keys[2], (NODES, WIDTH), 1.0, 6.0, ((0, 32),))
    adjacency = gaussian(keys[3], (ENTRIES, BLOCK, BLOCK), (4 * BLOCK) ** -0.5, 0.25, ((0, 32),))
    tile_row = set_ends(jax.random.randint(keys[4], (N_DOM, TILE_ENT), 0, TILES_DEV), jax.random.fold_in(keys[4], 1), 0, TILES_DEV - 1).astype(jnp.int32)
    tile_src = set_ends(jax.random.randint(keys[5], (N_DOM, TILE_ENT), 0, TILES_DEV + ROUNDS), jax.random.fold_in(keys[5], 1), 0, (TILES_DEV + ROUNDS) - 1).astype(jnp.int32)
    tile_count = draw_tile_count(jax.random.fold_in(keys[11], 71), 0)
    send_tile = set_ends(jax.random.randint(keys[7], (N_DOM, ROUNDS), 0, TILES_DEV), jax.random.fold_in(keys[7], 1), 0, TILES_DEV - 1).astype(jnp.int32)
    stale_feat = gaussian(keys[8], (N_DOM, ROUNDS, BLOCK, WIDTH), 1.0, 6.0, ((0, 32),))
    stale_grad = gaussian(keys[9], (N_DOM, ROUNDS, BLOCK, WIDTH), 1.0, 6.0, ((0, 32),))
    blend = jnp.clip(jax.random.uniform(keys[10], (WIDTH,), jnp.float32, 0.2, 0.8), 0.2, 0.8)
    return dict(features=features, weight=weight, grad_out=grad_out, adjacency=adjacency, tile_row=tile_row, tile_src=tile_src, tile_count=tile_count, send_tile=send_tile, stale_feat=stale_feat, stale_grad=stale_grad, blend=blend)


def forward_one(packed):
    table, adj_part, row_ids, src_ids, live_count = packed
    tiles_dev = NODES_DEV // BLOCK
    valid = (jnp.arange(TILE_ENT) < live_count).astype(jnp.float32)
    blocks = table[src_ids].astype(jnp.float32)
    product = jnp.einsum('ecb,ebh->ech', adj_part.astype(jnp.float32), blocks)
    onehot = (row_ids[:, None] == jnp.arange(tiles_dev)[None, :]).astype(jnp.float32) * valid[:, None]
    return jnp.einsum('et,ech->tch', onehot, product).astype(jnp.bfloat16)


def backward_one(packed):
    dz_part, adj_part, row_ids, src_ids, live_count = packed
    tiles_dev = NODES_DEV // BLOCK
    valid = (jnp.arange(TILE_ENT) < live_count).astype(jnp.float32)
    blocks = dz_part[row_ids].astype(jnp.float32)
    product = jnp.einsum('ecb,ech->ebh', adj_part.astype(jnp.float32), blocks)
    onehot = (src_ids[:, None] == jnp.arange(tiles_dev + ROUNDS)[None, :]).astype(jnp.float32) * valid[:, None]
    totals = jnp.einsum('es,ebh->sbh', onehot, product)
    return totals[:tiles_dev], totals[tiles_dev:].astype(jnp.bfloat16)


def reference(features, weight, grad_out, adjacency, tile_row, tile_src, tile_count, send_tile, stale_feat, stale_grad, blend):
    ndev = N_DOM
    tiles_dev = NODES_DEV // BLOCK
    nbits = ndev.bit_length() - 1
    devices = jnp.arange(ndev, dtype=jnp.int32)
    partners = jnp.stack([jnp.bitwise_xor(devices, jnp.int32(1 << (r * nbits // ROUNDS))) for r in range(ROUNDS)], 1)
    round_ids = jnp.arange(ROUNDS, dtype=jnp.int32)[None, :]
    node_tiles = features.reshape(ndev, tiles_dev, BLOCK, WIDTH)
    outgoing = node_tiles[devices[:, None], send_tile]
    fresh = outgoing[partners, round_ids].astype(jnp.float32)
    mixing = blend.astype(jnp.float32)
    used = ((1.0 - mixing) * stale_feat.astype(jnp.float32) + mixing * fresh).astype(jnp.bfloat16)
    table = jnp.concatenate([node_tiles, used], 1)
    adj_all = adjacency.reshape(ndev, TILE_ENT, BLOCK, BLOCK)
    agg = lax.map(forward_one, (table, adj_all, tile_row, tile_src, tile_count))
    agg_flat = agg.reshape(ndev * NODES_DEV, WIDTH)
    pre = jnp.dot(agg_flat, weight, preferred_element_type=jnp.float32)
    sigma = jax.nn.sigmoid(pre)
    output = (pre * sigma).astype(jnp.bfloat16)
    dpre = (grad_out.astype(jnp.float32) * sigma * (1.0 + pre * (1.0 - sigma))).astype(jnp.bfloat16)
    grad_weight = jnp.dot(agg_flat.T, dpre, preferred_element_type=jnp.float32).astype(jnp.bfloat16)
    dagg = jnp.dot(dpre, weight.T, preferred_element_type=jnp.float32).astype(jnp.bfloat16)
    dz_tiles = dagg.reshape(ndev, tiles_dev, BLOCK, WIDTH)
    local_part, sent = lax.map(backward_one, (dz_tiles, adj_all, tile_row, tile_src, tile_count))
    received = sent[partners, round_ids].astype(jnp.float32)
    corrected = (1.0 - mixing) * stale_grad.astype(jnp.float32) + mixing * received
    onehot_send = (send_tile[:, :, None] == jnp.arange(tiles_dev)[None, None, :]).astype(jnp.float32)
    grad_tiles = local_part + jnp.einsum('nrt,nrbh->ntbh', onehot_send, corrected)
    grad_features = grad_tiles.astype(jnp.bfloat16).reshape(ndev * NODES_DEV, WIDTH)
    return output, grad_features, grad_weight
```

```python
import functools

import jax
import jax.numpy as jnp
from jax import lax
from jax.experimental import pallas as pl
from jax.experimental.pallas import tpu as pltpu
from jax.sharding import PartitionSpec as P

MESH = pl.DeviceIdType.MESH
F32 = jnp.float32
BF16 = jnp.bfloat16
CHUNKS = 2
GROUP_BITS = 3
GROUP = 1 << GROUP_BITS
NEAR_LAST = (7, 6, 5, 3, 4, 2, 1)


def bit_of(i, b):
    return lax.rem(lax.div(i, 1 << b), 2)


class Index:
    def __init__(self, value, bits):
        self.value = value
        self.step = [(1 - 2 * bit_of(value, b)) * (1 << b) for b in range(bits)]

    def flip(self, mask):
        out = self.value
        for b in range(mask.bit_length()):
            if mask >> b & 1:
                out = out + self.step[b]
        return out


def upper_stages(nbits):
    stages, b = [], 1 + GROUP_BITS
    while b < nbits:
        stages.append((b, min(2, nbits - b)))
        b += 2
    return stages


def names_and_shapes(tiles, block, width, entries, rounds, n_upper):
    nodes = tiles * block
    half = width // 2
    piece = half // CHUNKS // GROUP
    v = pltpu.VMEM
    return dict(
        feat=v((tiles, block, width), BF16),
        wgt=v((width, width), BF16),
        gout=v((nodes, width), BF16),
        adj=v((entries, block, block), BF16),
        sfeat=v((rounds, block, width), BF16),
        sgrad=v((rounds * block, width), BF16),
        fsend=v((rounds, block, width), BF16),
        frecv=v((rounds, block, width), BF16),
        used=v((rounds * block, width), BF16),
        chain=v((entries + 1, block, block), F32),
        dense=v((nodes, (tiles + rounds) * block), BF16),
        pick=v((nodes, rounds * block), BF16),
        part=v((nodes, width), F32),
        aggt=v((width, nodes), BF16),
        outv=v((nodes, width), BF16),
        dpre=v((nodes, width), BF16),
        dagg=v((nodes, width), BF16),
        back=v((nodes, width), F32),
        gsend=v((rounds * block, width), BF16),
        grecv=v((rounds * block, width), BF16),
        gfeat=v((nodes, width), BF16),
        s0send=v((half, width), BF16),
        s0recv=v((half, width), BF16),
        acc=v((half, width), F32),
        s1send=v((half, width), BF16),
        s1recv=v((CHUNKS, (GROUP - 1) * piece, width), BF16),
        xbuf=v((max(n_upper, 1), CHUNKS, 4, piece, width), BF16),
        mine=v((CHUNKS, piece, width), BF16),
        mixv=v((1, width), F32),
        row_s=pltpu.SMEM((1, entries), jnp.int32),
        src_s=pltpu.SMEM((1, entries), jnp.int32),
        tile_s=pltpu.SMEM((1, rounds), jnp.int32),
        count_s=pltpu.SMEM((1, 1), jnp.int32),
        lsem=pltpu.SemaphoreType.DMA((11,)),
        ssem=pltpu.SemaphoreType.DMA((6 + n_upper,)),
        frsem=pltpu.SemaphoreType.DMA((rounds,)),
        grsem=pltpu.SemaphoreType.DMA((rounds,)),
        crsem=pltpu.SemaphoreType.DMA((CHUNKS,)),
        rrsem=pltpu.SemaphoreType.DMA((CHUNKS,)),
        xrsem=pltpu.SemaphoreType.DMA((max(n_upper, 1) * CHUNKS,)),
        arsem=pltpu.SemaphoreType.DMA((CHUNKS,)),
        trsem=pltpu.SemaphoreType.DMA((1,)),
    )


def kernel(names, nbits, *refs):
    (features, weight, grad_out, adjacency, stale_feat, stale_grad, blend,
     row_hbm, src_hbm, tile_hbm, count_hbm, out_any, gf_any, gw_any) = refs[:14]
    s = dict(zip(names, refs[14:]))
    send_tile = s["tile_s"]
    tiles, block, width = s["feat"].shape
    rounds = s["fsend"].shape[0]
    entries = s["adj"].shape[0]
    nodes = tiles * block
    cells = tiles + rounds
    half = width // 2
    chunk = half // CHUNKS
    piece = chunk // GROUP
    me = Index(lax.axis_index("dom"), nbits)
    core = bit_of(me.value, 0)
    spot = Index(lax.rem(lax.div(me.value, 2), GROUP), GROUP_BITS)
    upper = upper_stages(nbits)

    def remote(src, dst, send, recv, mask):
        pltpu.make_async_remote_copy(
            src_ref=src, dst_ref=dst, send_sem=send, recv_sem=recv,
            device_id=(me.flip(mask),), device_id_type=MESH).start()

    def settle(ref, sem):
        pltpu.make_async_copy(ref, ref, sem).wait()

    loads = {}
    for i, (src, name) in enumerate((
            (tile_hbm, "tile_s"), (features, "feat"), (row_hbm, "row_s"), (src_hbm, "src_s"),
            (count_hbm, "count_s"), (adjacency, "adj"), (blend, "mixv"), (stale_feat.at[0], "sfeat"),
            (weight, "wgt"), (grad_out, "gout"), (stale_grad, "sgrad"))):
        loads[name] = pltpu.make_async_copy(src, s[name], s["lsem"].at[i])
        loads[name].start()

    round_mask = [1 << (r * nbits // rounds) for r in range(rounds)]
    peers = {1} | {k << 1 for k in range(1, GROUP)} | set(round_mask)
    for lo, nb in upper:
        peers |= {k << lo for k in range(1, 1 << nb)}
    barrier = pltpu.get_barrier_semaphore()
    for m in sorted(peers):
        pl.semaphore_signal(barrier, inc=1, device_id=(me.flip(m),), device_id_type=MESH)

    early = [0] + list(range(3, rounds))
    late = [r for r in range(rounds) if r not in early]
    place = {r: i for i, r in enumerate(early + late)}
    loads["tile_s"].wait()
    loads["feat"].wait()
    for r in late + early[::-1]:
        s["fsend"][r] = s["feat"][send_tile[0, r]]
    pl.semaphore_wait(barrier, len(peers))
    for r in late + early[::-1]:
        remote(s["fsend"].at[r], s["frecv"].at[r], s["ssem"].at[0], s["frsem"].at[r], round_mask[r])

    for name in ("row_s", "src_s", "count_s"):
        loads[name].wait()
    live = s["count_s"][0, 0]
    keys = [jnp.where(e < live, s["row_s"][0, e] * cells + s["src_s"][0, e], -1 - e) for e in range(entries)]
    loads["adj"].wait()
    s["chain"][0] = jnp.zeros((block, block), F32)
    for e in range(entries):
        prev = jnp.int32(0)
        for f in range(e):
            prev = jnp.where(keys[f] == keys[e], f + 1, prev)
        s["chain"][e + 1] = s["chain"][prev] + s["adj"][e].astype(F32)
    for t in range(tiles):
        for c in range(cells):
            last = jnp.int32(0)
            for e in range(entries):
                last = jnp.where(keys[e] == t * cells + c, e + 1, last)
            at = c if c < tiles else tiles + place[c - tiles]
            s["dense"][t * block:(t + 1) * block, at * block:(at + 1) * block] = s["chain"][last].astype(BF16)

    loads["mixv"].wait()
    mix = s["mixv"][...]
    keep = 1.0 - mix
    s["part"][...] = jnp.dot(s["dense"][:, :nodes], s["feat"][...].reshape(nodes, width),
                             preferred_element_type=F32)
    eye = (lax.broadcasted_iota(jnp.int32, (block, block), 0)
           == lax.broadcasted_iota(jnp.int32, (block, block), 1)).astype(F32)
    for t in range(tiles):
        for r in range(rounds):
            hot = jnp.where(send_tile[0, r] == t, 1.0, 0.0).astype(F32)
            s["pick"][t * block:(t + 1) * block, r * block:(r + 1) * block] = (eye * hot).astype(BF16)
    loads["sfeat"].wait()
    loads["wgt"].wait()
    loads["gout"].wait()

    def blend_in(which):
        for r in which:
            pltpu.make_async_copy(s["frecv"].at[r], s["frecv"].at[r], s["frsem"].at[r]).wait()
            at = place[r]
            s["used"][at * block:(at + 1) * block, :] = (
                keep * s["sfeat"][r].astype(F32) + mix * s["frecv"][r].astype(F32)).astype(BF16)

    split = len(early) * block
    blend_in(early)
    s["part"][...] += jnp.dot(s["dense"][:, nodes:nodes + split], s["used"][:split, :],
                              preferred_element_type=F32)
    blend_in(late)
    step = 2 * block
    for t in range(nodes // step):
        rows = slice(t * step, (t + 1) * step)
        agg = (s["part"][rows, :] + jnp.dot(
            s["dense"][rows, nodes + split:], s["used"][split:, :],
            preferred_element_type=F32)).astype(BF16)
        s["aggt"][:, rows] = agg.T
        pre = jnp.dot(agg, s["wgt"][...], preferred_element_type=F32)
        sigma = jax.nn.sigmoid(pre)
        out = pre * sigma
        s["outv"][rows, :] = out.astype(BF16)
        s["dpre"][rows, :] = (s["gout"][rows, :].astype(F32) * sigma * (1.0 + pre * (1.0 - sigma))).astype(BF16)

    def half_product(h):
        return jnp.dot(s["aggt"][pl.ds(pl.multiple_of(h * half, half), half), :], s["dpre"][...],
                       preferred_element_type=F32)

    s["s0send"][...] = half_product(1 - core).astype(BF16)
    for q in range(CHUNKS):
        rows = pl.ds(q * chunk, chunk)
        remote(s["s0send"].at[rows], s["s0recv"].at[rows], s["ssem"].at[1], s["crsem"].at[q], 1)
    s["acc"][...] = half_product(core)
    out_copy = pltpu.make_async_copy(s["outv"], out_any, s["lsem"].at[0])
    out_copy.start()

    def own_rows(q, k=0):
        return pl.ds(pl.multiple_of(q * chunk + spot.flip(k) * piece, piece), piece)

    for q in range(CHUNKS):
        rows = slice(q * chunk, (q + 1) * chunk)
        settle(s["s0recv"].at[pl.ds(q * chunk, chunk)], s["crsem"].at[q])
        total = s["acc"][rows, :] + s["s0recv"][rows, :].astype(F32)
        s["acc"][rows, :] = total
        s["s1send"][rows, :] = total.astype(BF16)
        for k in NEAR_LAST:
            remote(s["s1send"].at[own_rows(q, k)], s["s1recv"].at[q, pl.ds((k - 1) * piece, piece)],
                   s["ssem"].at[2], s["rrsem"].at[q], k << 1)

    s["dagg"][...] = lax.dot_general(s["dpre"][...], s["wgt"][...], (((1,), (1,)), ((), ())),
                                     preferred_element_type=F32).astype(BF16)
    sent = lax.dot_general(s["dense"][:, nodes:], s["dagg"][...], (((0,), (0,)), ((), ())),
                           preferred_element_type=F32).astype(BF16)
    for r in range(rounds):
        s["gsend"][r * block:(r + 1) * block, :] = sent[place[r] * block:(place[r] + 1) * block, :]

    def send_back(r):
        rows = pl.ds(r * block, block)
        remote(s["gsend"].at[rows], s["grecv"].at[rows], s["ssem"].at[5], s["grsem"].at[r], round_mask[r])

    for r in early[:1]:
        send_back(r)
    loads["sgrad"].wait()
    s["back"][...] = lax.dot_general(s["dense"][:, :nodes], s["dagg"][...], (((0,), (0,)), ((), ())),
                                     preferred_element_type=F32) + keep * jnp.dot(
        s["pick"][...], s["sgrad"][...], preferred_element_type=F32)

    totals = []

    def swap(g, q, total):
        lo, nb = upper[g]
        at = lax.rem(lax.div(me.value, 1 << lo), 1 << nb)
        s["xbuf"][g, q, pl.ds(at, 1)] = total.astype(BF16)[None]
        for k in range(1, 1 << nb):
            remote(s["xbuf"].at[g, q, at], s["xbuf"].at[g, q, at], s["ssem"].at[6 + g],
                   s["xrsem"].at[g * CHUNKS + q], k << lo)

    def swapped(g, q):
        size = 1 << upper[g][1]
        settle(s["xbuf"].at[g, q, pl.ds(0, size - 1)], s["xrsem"].at[g * CHUNKS + q])
        total = s["xbuf"][g, q, 0].astype(F32)
        for x in range(1, size):
            total = total + s["xbuf"][g, q, x].astype(F32)
        return total

    def gw_rows(q):
        return pl.ds(pl.multiple_of(core * half + q * chunk + spot.value * piece, piece), piece)

    def spread(q, total):
        s["mine"][q] = total.astype(BF16)
        for k in NEAR_LAST:
            remote(s["mine"].at[q], gw_any.at[gw_rows(q)], s["ssem"].at[3], s["arsem"].at[q], k << 1)
        own = pltpu.make_async_copy(s["mine"].at[q], gw_any.at[gw_rows(q)], s["lsem"].at[1 + q])
        own.start()
        return own

    owns = []
    for q in range(CHUNKS):
        settle(s["s1recv"].at[q], s["rrsem"].at[q])
        total = s["acc"][own_rows(q), :]
        for k in range(1, GROUP):
            total = total + s["s1recv"][q, (k - 1) * piece:k * piece, :].astype(F32)
        if upper:
            swap(0, q, total)
        else:
            owns.append(spread(q, total))
    for r in range(rounds):
        if r not in early[:1]:
            send_back(r)
    for g in range(len(upper)):
        for q in range(CHUNKS):
            total = swapped(g, q)
            if g + 1 < len(upper):
                swap(g + 1, q, total)
            else:
                owns.append(spread(q, total))

    for r in range(rounds):
        rows = pl.ds(r * block, block)
        settle(s["grecv"].at[rows], s["grsem"].at[r])
    s["gfeat"][...] = (s["back"][...] + mix * jnp.dot(
        s["pick"][...], s["grecv"][...], preferred_element_type=F32)).astype(BF16)
    gf_copy = pltpu.make_async_copy(s["gfeat"], gf_any, s["lsem"].at[1 + CHUNKS])
    gf_copy.start()

    for q in range(CHUNKS):
        settle(s["s1recv"].at[q], s["arsem"].at[q])
        owns[q].wait()
        rows = pl.ds(pl.multiple_of(core * half + q * chunk, chunk), chunk)
        remote(gw_any.at[rows], gw_any.at[rows], s["ssem"].at[4], s["trsem"].at[0], 1)

    settle(s["fsend"], s["ssem"].at[0])
    settle(s["s0send"], s["ssem"].at[1])
    settle(s["s1recv"], s["ssem"].at[2])
    settle(s["s1recv"], s["ssem"].at[3])
    settle(s["gsend"], s["ssem"].at[5])
    for g, (lo, nb) in enumerate(upper):
        settle(s["xbuf"].at[g, :, pl.ds(0, (1 << nb) - 1)], s["ssem"].at[6 + g])
    out_copy.wait()
    gf_copy.wait()
    settle(s["s0recv"], s["trsem"].at[0])
    settle(s["s0recv"], s["ssem"].at[4])


def finish(*refs):
    ins, outs, sem = refs[:3], refs[3:6], refs[6]
    copies = [pltpu.make_async_copy(a, b, sem.at[i]) for i, (a, b) in enumerate(zip(ins, outs))]
    for c in copies:
        c.start()
    for c in copies:
        c.wait()


def body(nbits, features, weight, grad_out, adjacency, tile_row, tile_src, tile_count,
         send_tile, stale_feat, stale_grad, blend):
    nodes, width = features.shape
    entries, block = adjacency.shape[:2]
    rounds = send_tile.shape[1]
    tiles = nodes // block
    scratch = names_and_shapes(tiles, block, width, entries, rounds, len(upper_stages(nbits)))
    hbm = pl.BlockSpec(memory_space=pltpu.HBM)
    free = pl.BlockSpec(memory_space=pl.ANY)
    results = (jax.ShapeDtypeStruct((nodes, width), BF16),
               jax.ShapeDtypeStruct((nodes, width), BF16),
               jax.ShapeDtypeStruct((width, width), BF16))
    found = pl.pallas_call(
        functools.partial(kernel, tuple(scratch), nbits),
        name="layer",
        out_shape=results,
        in_specs=[hbm] * 10 + [free],
        out_specs=(free,) * 3,
        scratch_shapes=list(scratch.values()),
        compiler_params=pltpu.CompilerParams(collective_id=0, has_side_effects=True,
                                             vmem_limit_bytes=48 * 1024 * 1024),
    )(*(pltpu.with_memory_space_constraint(x, pltpu.HBM) for x in (
        features.reshape(tiles, block, width), weight, grad_out, adjacency, stale_feat,
        stale_grad.reshape(rounds * block, width), blend.reshape(1, width),
        tile_row, tile_src, send_tile)), tile_count.reshape(1, 1))
    return tuple(pl.pallas_call(
        finish,
        name="finish",
        out_shape=results,
        in_specs=[free] * 3,
        out_specs=(hbm,) * 3,
        scratch_shapes=[pltpu.SemaphoreType.DMA((3,))],
        compiler_params=pltpu.CompilerParams(vmem_limit_bytes=16 * 1024 * 1024),
    )(*found))


def solution(mesh):
    nbits = mesh.shape["dom"].bit_length() - 1
    placed = (
        P("dom", None), P(), P("dom", None), P("dom", None, None), P("dom", None), P("dom", None),
        P("dom"), P("dom", None), P("dom", None, None, None), P("dom", None, None, None), P(),
    )
    return jax.shard_map(
        functools.partial(body, nbits),
        mesh=mesh,
        in_specs=placed,
        out_specs=(P("dom", None), P("dom", None), P()),
        check_vma=False,
    )
```

```python
import functools

import jax
import jax.numpy as jnp
from jax import lax
from jax.experimental import pallas as pl
from jax.experimental.pallas import tpu as pltpu
from jax.sharding import PartitionSpec as P

MESH = pl.DeviceIdType.MESH
F32 = jnp.float32
BF16 = jnp.bfloat16
CHUNKS = 2
GROUP_BITS = 3
GROUP = 1 << GROUP_BITS
NEAR_LAST = (7, 6, 5, 3, 4, 2, 1)


def bit_of(i, b):
    return lax.rem(lax.div(i, 1 << b), 2)


class Index:
    def __init__(self, value, bits):
        self.value = value
        self.step = [(1 - 2 * bit_of(value, b)) * (1 << b) for b in range(bits)]

    def flip(self, mask):
        out = self.value
        for b in range(mask.bit_length()):
            if mask >> b & 1:
                out = out + self.step[b]
        return out


def upper_stages(nbits):
    stages, b = [], 1 + GROUP_BITS
    while b < nbits:
        stages.append((b, min(2, nbits - b)))
        b += 2
    return stages


def names_and_shapes(tiles, block, width, entries, rounds, n_upper):
    nodes = tiles * block
    half = width // 2
    piece = half // CHUNKS // GROUP
    v = pltpu.VMEM
    return dict(
        feat=v((tiles, block, width), BF16),
        wgt=v((width, width), BF16),
        gout=v((nodes, width), BF16),
        adj=v((entries, block, block), BF16),
        sfeat=v((rounds, block, width), BF16),
        sgrad=v((rounds * block, width), BF16),
        fsend=v((rounds, block, width), BF16),
        frecv=v((rounds, block, width), BF16),
        used=v((rounds * block, width), BF16),
        chain=v((entries + 1, block, block), F32),
        dense=v((nodes, (tiles + rounds) * block), BF16),
        pick=v((nodes, rounds * block), BF16),
        edge=v((rounds * block, nodes), BF16),
        wgtt=v((width, width), BF16),
        part=v((nodes, width), F32),
        aggt=v((width, nodes), BF16),
        dpre=v((nodes, width), BF16),
        dagg=v((nodes, width), BF16),
        back=v((nodes, width), F32),
        gsend=v((rounds * block, width), BF16),
        grecv=v((rounds * block, width), BF16),
        s0send=v((half, width), BF16),
        s0recv=v((half, width), BF16),
        acc=v((half, width), F32),
        s1send=v((half, width), BF16),
        s1recv=v((CHUNKS, (GROUP - 1) * piece, width), BF16),
        xbuf=v((max(n_upper, 1), CHUNKS, 4, piece, width), BF16),
        mine=v((CHUNKS, piece, width), BF16),
        mixv=v((1, width), F32),
        row_s=pltpu.SMEM((1, entries), jnp.int32),
        src_s=pltpu.SMEM((1, entries), jnp.int32),
        tile_s=pltpu.SMEM((1, rounds), jnp.int32),
        count_s=pltpu.SMEM((1, 1), jnp.int32),
        lsem=pltpu.SemaphoreType.DMA((11,)),
        ssem=pltpu.SemaphoreType.DMA((6 + n_upper,)),
        frsem=pltpu.SemaphoreType.DMA((rounds,)),
        grsem=pltpu.SemaphoreType.DMA((rounds,)),
        crsem=pltpu.SemaphoreType.DMA((CHUNKS,)),
        rrsem=pltpu.SemaphoreType.DMA((CHUNKS,)),
        xrsem=pltpu.SemaphoreType.DMA((max(n_upper, 1) * CHUNKS,)),
        arsem=pltpu.SemaphoreType.DMA((CHUNKS,)),
        trsem=pltpu.SemaphoreType.DMA((1,)),
    )


def kernel(names, nbits, *refs):
    (features, weight, grad_out, adjacency, stale_feat, stale_grad, blend,
     row_hbm, src_hbm, tile_hbm, count_hbm, out_any, gf_any, gw_any) = refs[:14]
    s = dict(zip(names, refs[14:]))
    send_tile = s["tile_s"]
    tiles, block, width = s["feat"].shape
    rounds = s["fsend"].shape[0]
    entries = s["adj"].shape[0]
    nodes = tiles * block
    cells = tiles + rounds
    half = width // 2
    chunk = half // CHUNKS
    piece = chunk // GROUP
    me = Index(lax.axis_index("dom"), nbits)
    core = bit_of(me.value, 0)
    spot = Index(lax.rem(lax.div(me.value, 2), GROUP), GROUP_BITS)
    upper = upper_stages(nbits)

    def remote(src, dst, send, recv, mask):
        pltpu.make_async_remote_copy(
            src_ref=src, dst_ref=dst, send_sem=send, recv_sem=recv,
            device_id=(me.flip(mask),), device_id_type=MESH).start()

    def settle(ref, sem):
        pltpu.make_async_copy(ref, ref, sem).wait()

    round_mask = [1 << (r * nbits // rounds) for r in range(rounds)]
    peers = {1} | {k << 1 for k in range(1, GROUP)} | set(round_mask)
    for lo, nb in upper:
        peers |= {k << lo for k in range(1, 1 << nb)}
    barrier = pltpu.get_barrier_semaphore()
    for m in sorted(peers):
        pl.semaphore_signal(barrier, inc=1, device_id=(me.flip(m),), device_id_type=MESH)

    loads = {}
    for i, (src, name) in enumerate((
            (tile_hbm, "tile_s"), (features, "feat"), (row_hbm, "row_s"), (src_hbm, "src_s"),
            (count_hbm, "count_s"), (adjacency, "adj"), (blend, "mixv"), (stale_feat.at[0], "sfeat"),
            (weight, "wgt"), (grad_out, "gout"), (stale_grad, "sgrad"))):
        loads[name] = pltpu.make_async_copy(src, s[name], s["lsem"].at[i])
        loads[name].start()

    early = [0] + list(range(3, rounds))
    late = [r for r in range(rounds) if r not in early]
    place = {r: i for i, r in enumerate(early + late)}
    loads["tile_s"].wait()
    loads["feat"].wait()
    for r in late + early[::-1]:
        s["fsend"][r] = s["feat"][send_tile[0, r]]
    pl.semaphore_wait(barrier, len(peers))
    for r in late + early[::-1]:
        remote(s["fsend"].at[r], s["frecv"].at[r], s["ssem"].at[0], s["frsem"].at[r], round_mask[r])

    for name in ("row_s", "src_s", "count_s"):
        loads[name].wait()
    live = s["count_s"][0, 0]
    keys = [jnp.where(e < live, s["row_s"][0, e] * cells + s["src_s"][0, e], -1 - e) for e in range(entries)]
    loads["adj"].wait()
    s["chain"][0] = jnp.zeros((block, block), F32)
    for e in range(entries):
        prev = jnp.int32(0)
        for f in range(e):
            prev = jnp.where(keys[f] == keys[e], f + 1, prev)
        s["chain"][e + 1] = s["chain"][prev] + s["adj"][e].astype(F32)
    for t in range(tiles):
        for c in range(cells):
            last = jnp.int32(0)
            for e in range(entries):
                last = jnp.where(keys[e] == t * cells + c, e + 1, last)
            at = c if c < tiles else tiles + place[c - tiles]
            cell = s["chain"][last].astype(BF16)
            s["dense"][t * block:(t + 1) * block, at * block:(at + 1) * block] = cell
            if c >= tiles:
                s["edge"][(c - tiles) * block:(c - tiles + 1) * block, t * block:(t + 1) * block] = cell.T

    loads["mixv"].wait()
    mix = s["mixv"][...]
    keep = 1.0 - mix
    s["part"][...] = jnp.dot(s["dense"][:, :nodes], s["feat"][...].reshape(nodes, width),
                             preferred_element_type=F32)
    eye = (lax.broadcasted_iota(jnp.int32, (block, block), 0)
           == lax.broadcasted_iota(jnp.int32, (block, block), 1)).astype(F32)
    for t in range(tiles):
        for r in range(rounds):
            hot = jnp.where(send_tile[0, r] == t, 1.0, 0.0).astype(F32)
            s["pick"][t * block:(t + 1) * block, r * block:(r + 1) * block] = (eye * hot).astype(BF16)
    loads["sfeat"].wait()
    loads["wgt"].wait()
    s["wgtt"][...] = s["wgt"][...].T
    loads["gout"].wait()

    def blend_in(which):
        for r in which:
            pltpu.make_async_copy(s["frecv"].at[r], s["frecv"].at[r], s["frsem"].at[r]).wait()
            at = place[r]
            s["used"][at * block:(at + 1) * block, :] = (
                keep * s["sfeat"][r].astype(F32) + mix * s["frecv"][r].astype(F32)).astype(BF16)

    split = len(early) * block
    blend_in(early)
    s["part"][...] += jnp.dot(s["dense"][:, nodes:nodes + split], s["used"][:split, :],
                              preferred_element_type=F32)
    blend_in(late)
    step = 2 * block
    for t in range(nodes // step):
        rows = slice(t * step, (t + 1) * step)
        agg = (s["part"][rows, :] + jnp.dot(
            s["dense"][rows, nodes + split:], s["used"][split:, :],
            preferred_element_type=F32)).astype(BF16)
        s["aggt"][:, rows] = agg.T
        pre = jnp.dot(agg, s["wgt"][...], preferred_element_type=F32)
        sigma = jax.nn.sigmoid(pre)
        out = pre * sigma
        out_any[rows, :] = out.astype(BF16)
        s["dpre"][rows, :] = (s["gout"][rows, :].astype(F32) * sigma * (1.0 + pre * (1.0 - sigma))).astype(BF16)

    def chunk_product(h, q):
        return jnp.dot(s["aggt"][pl.ds(pl.multiple_of(h * half + q * chunk, chunk), chunk), :], s["dpre"][...],
                       preferred_element_type=F32)

    for q in range(CHUNKS):
        rows = pl.ds(q * chunk, chunk)
        s["s0send"][q * chunk:(q + 1) * chunk, :] = chunk_product(1 - core, q).astype(BF16)
        remote(s["s0send"].at[rows], s["s0recv"].at[rows], s["ssem"].at[1], s["crsem"].at[q], 1)
    for q in range(CHUNKS):
        s["acc"][q * chunk:(q + 1) * chunk, :] = chunk_product(core, q)

    def send_back(r):
        rows = pl.ds(r * block, block)
        remote(s["gsend"].at[rows], s["grecv"].at[rows], s["ssem"].at[5], s["grsem"].at[r], round_mask[r])

    def make_back():
        s["dagg"][...] = jnp.dot(s["dpre"][...], s["wgtt"][...], preferred_element_type=F32).astype(BF16)
        s["gsend"][...] = jnp.dot(s["edge"][...], s["dagg"][...], preferred_element_type=F32).astype(BF16)

    @pl.when(core == 1)
    def _():
        make_back()
        for r in late + early[::-1]:
            send_back(r)

    def own_rows(q, k=0):
        return pl.ds(pl.multiple_of(q * chunk + spot.flip(k) * piece, piece), piece)

    for q in range(CHUNKS):
        rows = slice(q * chunk, (q + 1) * chunk)
        settle(s["s0recv"].at[pl.ds(q * chunk, chunk)], s["crsem"].at[q])
        total = s["acc"][rows, :] + s["s0recv"][rows, :].astype(F32)
        s["acc"][rows, :] = total
        s["s1send"][rows, :] = total.astype(BF16)
        for k in NEAR_LAST:
            remote(s["s1send"].at[own_rows(q, k)], s["s1recv"].at[q, pl.ds((k - 1) * piece, piece)],
                   s["ssem"].at[2], s["rrsem"].at[q], k << 1)

    @pl.when(core == 0)
    def _():
        make_back()
        for r in early[:1]:
            send_back(r)

    loads["sgrad"].wait()
    s["back"][...] = lax.dot_general(s["dense"][:, :nodes], s["dagg"][...], (((0,), (0,)), ((), ())),
                                     preferred_element_type=F32) + keep * jnp.dot(
        s["pick"][...], s["sgrad"][...], preferred_element_type=F32)

    totals = []

    def swap(g, q, total):
        lo, nb = upper[g]
        at = lax.rem(lax.div(me.value, 1 << lo), 1 << nb)
        s["xbuf"][g, q, pl.ds(at, 1)] = total.astype(BF16)[None]
        for k in range(1, 1 << nb):
            remote(s["xbuf"].at[g, q, at], s["xbuf"].at[g, q, at], s["ssem"].at[6 + g],
                   s["xrsem"].at[g * CHUNKS + q], k << lo)

    def swapped(g, q):
        size = 1 << upper[g][1]
        settle(s["xbuf"].at[g, q, pl.ds(0, size - 1)], s["xrsem"].at[g * CHUNKS + q])
        total = s["xbuf"][g, q, 0].astype(F32)
        for x in range(1, size):
            total = total + s["xbuf"][g, q, x].astype(F32)
        return total

    def gw_rows(q):
        return pl.ds(pl.multiple_of(core * half + q * chunk + spot.value * piece, piece), piece)

    def spread(q, total):
        s["mine"][q] = total.astype(BF16)
        for k in NEAR_LAST:
            remote(s["mine"].at[q], gw_any.at[gw_rows(q)], s["ssem"].at[3], s["arsem"].at[q], k << 1)
        own = pltpu.make_async_copy(s["mine"].at[q], gw_any.at[gw_rows(q)], s["lsem"].at[1 + q])
        own.start()
        return own

    owns = []
    for q in range(CHUNKS):
        settle(s["s1recv"].at[q], s["rrsem"].at[q])
        total = s["acc"][own_rows(q), :]
        for k in range(1, GROUP):
            total = total + s["s1recv"][q, (k - 1) * piece:k * piece, :].astype(F32)
        if upper:
            swap(0, q, total)
        else:
            owns.append(spread(q, total))
    @pl.when(core == 0)
    def _():
        for r in late + early[:0:-1]:
            send_back(r)

    for g in range(len(upper)):
        for q in range(CHUNKS):
            total = swapped(g, q)
            if g + 1 < len(upper):
                swap(g + 1, q, total)
            else:
                owns.append(spread(q, total))

    for r in range(rounds):
        rows = pl.ds(r * block, block)
        settle(s["grecv"].at[rows], s["grsem"].at[r])
    gf_any[...] = (s["back"][...] + mix * jnp.dot(
        s["pick"][...], s["grecv"][...], preferred_element_type=F32)).astype(BF16)

    for q in range(CHUNKS):
        settle(s["s1recv"].at[q], s["arsem"].at[q])
        owns[q].wait()
        rows = pl.ds(pl.multiple_of(core * half + q * chunk, chunk), chunk)
        remote(gw_any.at[rows], gw_any.at[rows], s["ssem"].at[4], s["trsem"].at[0], 1)

    settle(s["fsend"], s["ssem"].at[0])
    settle(s["s0send"], s["ssem"].at[1])
    settle(s["s1recv"], s["ssem"].at[2])
    settle(s["s1recv"], s["ssem"].at[3])
    settle(s["gsend"], s["ssem"].at[5])
    for g, (lo, nb) in enumerate(upper):
        settle(s["xbuf"].at[g, :, pl.ds(0, (1 << nb) - 1)], s["ssem"].at[6 + g])
    settle(s["s0recv"], s["trsem"].at[0])
    settle(s["s0recv"], s["ssem"].at[4])


def finish(*refs):
    ins, outs, sem = refs[:3], refs[3:6], refs[6]
    copies = [pltpu.make_async_copy(a, b, sem.at[i]) for i, (a, b) in enumerate(zip(ins, outs))]
    for c in copies:
        c.start()
    for c in copies:
        c.wait()


def body(nbits, features, weight, grad_out, adjacency, tile_row, tile_src, tile_count,
         send_tile, stale_feat, stale_grad, blend):
    nodes, width = features.shape
    entries, block = adjacency.shape[:2]
    rounds = send_tile.shape[1]
    tiles = nodes // block
    scratch = names_and_shapes(tiles, block, width, entries, rounds, len(upper_stages(nbits)))
    hbm = pl.BlockSpec(memory_space=pltpu.HBM)
    free = pl.BlockSpec(memory_space=pl.ANY)
    results = (jax.ShapeDtypeStruct((nodes, width), BF16),
               jax.ShapeDtypeStruct((nodes, width), BF16),
               jax.ShapeDtypeStruct((width, width), BF16))
    found = pl.pallas_call(
        functools.partial(kernel, tuple(scratch), nbits),
        name="layer",
        out_shape=results,
        in_specs=[hbm] * 10 + [free],
        out_specs=(pl.BlockSpec(memory_space=pltpu.VMEM),) * 2 + (free,),
        scratch_shapes=list(scratch.values()),
        compiler_params=pltpu.CompilerParams(collective_id=0, has_side_effects=True,
                                             vmem_limit_bytes=48 * 1024 * 1024),
    )(*(pltpu.with_memory_space_constraint(x, pltpu.HBM) for x in (
        features.reshape(tiles, block, width), weight, grad_out, adjacency, stale_feat,
        stale_grad.reshape(rounds * block, width), blend.reshape(1, width),
        tile_row, tile_src, send_tile)), tile_count.reshape(1, 1))
    return tuple(pl.pallas_call(
        finish,
        name="finish",
        out_shape=results,
        in_specs=[free] * 3,
        out_specs=(hbm,) * 3,
        scratch_shapes=[pltpu.SemaphoreType.DMA((3,))],
        compiler_params=pltpu.CompilerParams(vmem_limit_bytes=16 * 1024 * 1024),
    )(*found))


def solution(mesh):
    nbits = mesh.shape["dom"].bit_length() - 1
    placed = (
        P("dom", None), P(), P("dom", None), P("dom", None, None), P("dom", None), P("dom", None),
        P("dom"), P("dom", None), P("dom", None, None, None), P("dom", None, None, None), P(),
    )
    return jax.shard_map(
        functools.partial(body, nbits),
        mesh=mesh,
        in_specs=placed,
        out_specs=(P("dom", None), P("dom", None), P()),
        check_vma=False,
    )
```

```python
import functools

import jax
import jax.numpy as jnp
from jax import lax
from jax.experimental import pallas as pl
from jax.experimental.pallas import tpu as pltpu
from jax.sharding import PartitionSpec as P

MESH = pl.DeviceIdType.MESH
F32 = jnp.float32
BF16 = jnp.bfloat16
CHUNKS = 2
GROUP_BITS = 3
GROUP = 1 << GROUP_BITS
NEAR_LAST = (7, 6, 5, 3, 4, 2, 1)


def bit_of(i, b):
    return lax.rem(lax.div(i, 1 << b), 2)


class Index:
    def __init__(self, value, bits):
        self.value = value
        self.step = [(1 - 2 * bit_of(value, b)) * (1 << b) for b in range(bits)]

    def flip(self, mask):
        out = self.value
        for b in range(mask.bit_length()):
            if mask >> b & 1:
                out = out + self.step[b]
        return out


def upper_stages(nbits):
    stages, b = [], 1 + GROUP_BITS
    while b < nbits:
        stages.append((b, min(2, nbits - b)))
        b += 2
    return stages


def names_and_shapes(tiles, block, width, entries, rounds, n_upper):
    nodes = tiles * block
    half = width // 2
    piece = half // CHUNKS // GROUP
    v = pltpu.VMEM
    return dict(
        feat=v((tiles, block, width), BF16),
        wgt=v((width, width), BF16),
        gout=v((nodes, width), BF16),
        adj=v((entries, block, block), BF16),
        sfeat=v((rounds, block, width), BF16),
        sgrad=v((rounds * block, width), BF16),
        fsend=v((rounds, block, width), BF16),
        frecv=v((rounds, block, width), BF16),
        used=v((rounds * block, width), BF16),
        chain=v((entries + 1, block, block), F32),
        dense=v((nodes, (tiles + rounds) * block), BF16),
        pick=v((nodes, rounds * block), BF16),
        edge=v((rounds * block, nodes), BF16),
        wgtt=v((width, width), BF16),
        part=v((nodes, width), F32),
        aggt=v((width, nodes), BF16),
        dpre=v((nodes, width), BF16),
        dagg=v((nodes, width), BF16),
        back=v((nodes, width), F32),
        gsend=v((rounds * block, width), BF16),
        grecv=v((rounds * block, width), BF16),
        s0send=v((half, width), BF16),
        s0recv=v((half, width), BF16),
        acc=v((half, width), F32),
        s1send=v((half, width), BF16),
        s1recv=v((CHUNKS, (GROUP - 1) * piece, width), BF16),
        xbuf=v((max(n_upper, 1), CHUNKS, 4, piece, width), BF16),
        mine=v((CHUNKS, piece, width), BF16),
        mixv=v((1, width), F32),
        row_s=pltpu.SMEM((1, entries), jnp.int32),
        src_s=pltpu.SMEM((1, entries), jnp.int32),
        tile_s=pltpu.SMEM((1, rounds), jnp.int32),
        count_s=pltpu.SMEM((1, 1), jnp.int32),
        lsem=pltpu.SemaphoreType.DMA((11,)),
        ssem=pltpu.SemaphoreType.DMA((6 + n_upper,)),
        frsem=pltpu.SemaphoreType.DMA((rounds,)),
        grsem=pltpu.SemaphoreType.DMA((1,)),
        crsem=pltpu.SemaphoreType.DMA((CHUNKS,)),
        rrsem=pltpu.SemaphoreType.DMA((CHUNKS,)),
        xrsem=pltpu.SemaphoreType.DMA((max(n_upper, 1) * CHUNKS,)),
        arsem=pltpu.SemaphoreType.DMA((CHUNKS - 1 + GROUP - 1,)),
        trsem=pltpu.SemaphoreType.DMA((1,)),
    )


def kernel(names, nbits, *refs):
    (features, weight, grad_out, adjacency, stale_feat, stale_grad, blend,
     row_hbm, src_hbm, tile_hbm, count_hbm, out_any, gf_any, gw_any) = refs[:14]
    s = dict(zip(names, refs[14:]))
    send_tile = s["tile_s"]
    tiles, block, width = s["feat"].shape
    rounds = s["fsend"].shape[0]
    entries = s["adj"].shape[0]
    nodes = tiles * block
    cells = tiles + rounds
    half = width // 2
    chunk = half // CHUNKS
    piece = chunk // GROUP
    me = Index(lax.axis_index("dom"), nbits)
    core = bit_of(me.value, 0)
    spot = Index(lax.rem(lax.div(me.value, 2), GROUP), GROUP_BITS)
    upper = upper_stages(nbits)

    def remote(src, dst, send, recv, mask):
        pltpu.make_async_remote_copy(
            src_ref=src, dst_ref=dst, send_sem=send, recv_sem=recv,
            device_id=(me.flip(mask),), device_id_type=MESH).start()

    def settle(ref, sem):
        pltpu.make_async_copy(ref, ref, sem).wait()

    round_mask = [1 << (r * nbits // rounds) for r in range(rounds)]
    peers = {1} | {k << 1 for k in range(1, GROUP)} | set(round_mask)
    for lo, nb in upper:
        peers |= {k << lo for k in range(1, 1 << nb)}
    barrier = pltpu.get_barrier_semaphore()
    for m in sorted(peers):
        pl.semaphore_signal(barrier, inc=1, device_id=(me.flip(m),), device_id_type=MESH)

    loads = {}
    for i, (src, name) in enumerate((
            (tile_hbm, "tile_s"), (features, "feat"), (row_hbm, "row_s"), (src_hbm, "src_s"),
            (count_hbm, "count_s"), (adjacency, "adj"), (blend, "mixv"), (stale_feat.at[0], "sfeat"),
            (weight, "wgt"), (grad_out, "gout"), (stale_grad, "sgrad"))):
        loads[name] = pltpu.make_async_copy(src, s[name], s["lsem"].at[i])
        loads[name].start()

    early = [0] + list(range(3, rounds))
    late = [r for r in range(rounds) if r not in early]
    place = {r: i for i, r in enumerate(early + late)}
    loads["tile_s"].wait()
    loads["feat"].wait()
    for r in late + early[::-1]:
        s["fsend"][r] = s["feat"][send_tile[0, r]]
    pl.semaphore_wait(barrier, len(peers))
    for r in late + early[::-1]:
        remote(s["fsend"].at[r], s["frecv"].at[r], s["ssem"].at[0], s["frsem"].at[r], round_mask[r])

    for name in ("row_s", "src_s", "count_s"):
        loads[name].wait()
    live = s["count_s"][0, 0]
    keys = [jnp.where(e < live, s["row_s"][0, e] * cells + s["src_s"][0, e], -1 - e) for e in range(entries)]
    loads["adj"].wait()
    s["chain"][0] = jnp.zeros((block, block), F32)
    for e in range(entries):
        prev = jnp.int32(0)
        for f in range(e):
            prev = jnp.where(keys[f] == keys[e], f + 1, prev)
        s["chain"][e + 1] = s["chain"][prev] + s["adj"][e].astype(F32)
    for t in range(tiles):
        for c in range(cells):
            last = jnp.int32(0)
            for e in range(entries):
                last = jnp.where(keys[e] == t * cells + c, e + 1, last)
            at = c if c < tiles else tiles + place[c - tiles]
            cell = s["chain"][last].astype(BF16)
            s["dense"][t * block:(t + 1) * block, at * block:(at + 1) * block] = cell
            if c >= tiles:
                s["edge"][(c - tiles) * block:(c - tiles + 1) * block, t * block:(t + 1) * block] = cell.T

    loads["mixv"].wait()
    mix = s["mixv"][...]
    keep = 1.0 - mix
    s["part"][...] = jnp.dot(s["dense"][:, :nodes], s["feat"][...].reshape(nodes, width),
                             preferred_element_type=F32)
    eye = (lax.broadcasted_iota(jnp.int32, (block, block), 0)
           == lax.broadcasted_iota(jnp.int32, (block, block), 1)).astype(F32)
    for t in range(tiles):
        for r in range(rounds):
            hot = jnp.where(send_tile[0, r] == t, 1.0, 0.0).astype(F32)
            s["pick"][t * block:(t + 1) * block, r * block:(r + 1) * block] = (eye * hot).astype(BF16)
    loads["sfeat"].wait()
    loads["wgt"].wait()
    s["wgtt"][...] = s["wgt"][...].T
    loads["gout"].wait()

    def blend_in(which):
        for r in which:
            pltpu.make_async_copy(s["frecv"].at[r], s["frecv"].at[r], s["frsem"].at[r]).wait()
            at = place[r]
            s["used"][at * block:(at + 1) * block, :] = (
                keep * s["sfeat"][r].astype(F32) + mix * s["frecv"][r].astype(F32)).astype(BF16)

    split = len(early) * block
    blend_in(early)
    s["part"][...] += jnp.dot(s["dense"][:, nodes:nodes + split], s["used"][:split, :],
                              preferred_element_type=F32)
    blend_in(late)
    step = 2 * block
    for t in range(nodes // step):
        rows = slice(t * step, (t + 1) * step)
        agg = (s["part"][rows, :] + jnp.dot(
            s["dense"][rows, nodes + split:], s["used"][split:, :],
            preferred_element_type=F32)).astype(BF16)
        s["aggt"][:, rows] = agg.T
        pre = jnp.dot(agg, s["wgt"][...], preferred_element_type=F32)
        sigma = jax.nn.sigmoid(pre)
        out = pre * sigma
        out_any[rows, :] = out.astype(BF16)
        s["dpre"][rows, :] = (s["gout"][rows, :].astype(F32) * sigma * (1.0 + pre * (1.0 - sigma))).astype(BF16)

    def chunk_product(h, q):
        return jnp.dot(s["aggt"][pl.ds(pl.multiple_of(h * half + q * chunk, chunk), chunk), :], s["dpre"][...],
                       preferred_element_type=F32)

    for q in range(CHUNKS):
        rows = pl.ds(q * chunk, chunk)
        s["s0send"][q * chunk:(q + 1) * chunk, :] = chunk_product(1 - core, q).astype(BF16)
        remote(s["s0send"].at[rows], s["s0recv"].at[rows], s["ssem"].at[1], s["crsem"].at[q], 1)
    for q in range(CHUNKS):
        s["acc"][q * chunk:(q + 1) * chunk, :] = chunk_product(core, q)

    def send_back(r):
        rows = pl.ds(r * block, block)
        remote(s["gsend"].at[rows], s["grecv"].at[rows], s["ssem"].at[5], s["grsem"].at[0], round_mask[r])

    def make_back():
        s["dagg"][...] = jnp.dot(s["dpre"][...], s["wgtt"][...], preferred_element_type=F32).astype(BF16)
        s["gsend"][...] = jnp.dot(s["edge"][...], s["dagg"][...], preferred_element_type=F32).astype(BF16)

    @pl.when(core == 1)
    def _():
        make_back()
        for r in late + early[::-1]:
            send_back(r)

    def own_rows(q, k=0):
        return pl.ds(pl.multiple_of(q * chunk + spot.flip(k) * piece, piece), piece)

    for q in range(CHUNKS):
        rows = slice(q * chunk, (q + 1) * chunk)
        settle(s["s0recv"].at[pl.ds(q * chunk, chunk)], s["crsem"].at[q])
        total = s["acc"][rows, :] + s["s0recv"][rows, :].astype(F32)
        s["acc"][rows, :] = total
        s["s1send"][rows, :] = total.astype(BF16)
        for k in NEAR_LAST:
            remote(s["s1send"].at[own_rows(q, k)], s["s1recv"].at[q, pl.ds((k - 1) * piece, piece)],
                   s["ssem"].at[2], s["rrsem"].at[q], k << 1)

    @pl.when(core == 0)
    def _():
        make_back()
        for r in early[:1]:
            send_back(r)

    loads["sgrad"].wait()
    s["back"][...] = lax.dot_general(s["dense"][:, :nodes], s["dagg"][...], (((0,), (0,)), ((), ())),
                                     preferred_element_type=F32) + keep * jnp.dot(
        s["pick"][...], s["sgrad"][...], preferred_element_type=F32)

    totals = []

    def swap(g, q, total):
        lo, nb = upper[g]
        at = lax.rem(lax.div(me.value, 1 << lo), 1 << nb)
        s["xbuf"][g, q, pl.ds(at, 1)] = total.astype(BF16)[None]
        for k in range(1, 1 << nb):
            remote(s["xbuf"].at[g, q, at], s["xbuf"].at[g, q, at], s["ssem"].at[6 + g],
                   s["xrsem"].at[g * CHUNKS + q], k << lo)

    def swapped(g, q):
        size = 1 << upper[g][1]
        settle(s["xbuf"].at[g, q, pl.ds(0, size - 1)], s["xrsem"].at[g * CHUNKS + q])
        total = s["xbuf"][g, q, 0].astype(F32)
        for x in range(1, size):
            total = total + s["xbuf"][g, q, x].astype(F32)
        return total

    def gw_rows(q):
        return pl.ds(pl.multiple_of(core * half + q * chunk + spot.value * piece, piece), piece)

    def spread(q, total):
        s["mine"][q] = total.astype(BF16)
        for k in NEAR_LAST:
            remote(s["mine"].at[q], gw_any.at[gw_rows(q)], s["ssem"].at[3],
                   s["arsem"].at[q if q < CHUNKS - 1 else q + k - 1], k << 1)
        own = pltpu.make_async_copy(s["mine"].at[q], gw_any.at[gw_rows(q)], s["lsem"].at[1 + q])
        own.start()
        return own

    owns = []
    for q in range(CHUNKS):
        settle(s["s1recv"].at[q], s["rrsem"].at[q])
        total = s["acc"][own_rows(q), :]
        for k in range(1, GROUP):
            total = total + s["s1recv"][q, (k - 1) * piece:k * piece, :].astype(F32)
        if upper:
            swap(0, q, total)
        else:
            owns.append(spread(q, total))
    @pl.when(core == 0)
    def _():
        for r in late + early[:0:-1]:
            send_back(r)

    for g in range(len(upper)):
        for q in range(CHUNKS):
            total = swapped(g, q)
            if g + 1 < len(upper):
                swap(g + 1, q, total)
            else:
                owns.append(spread(q, total))

    settle(s["grecv"], s["grsem"].at[0])
    gf_any[...] = (s["back"][...] + mix * jnp.dot(
        s["pick"][...], s["grecv"][...], preferred_element_type=F32)).astype(BF16)

    for q in range(CHUNKS - 1):
        settle(s["s1recv"].at[q], s["arsem"].at[q])
        owns[q].wait()
        rows = pl.ds(pl.multiple_of(core * half + q * chunk, chunk), chunk)
        remote(gw_any.at[rows], gw_any.at[rows], s["ssem"].at[4], s["trsem"].at[0], 1)
    q = CHUNKS - 1
    for k in (0,) + NEAR_LAST[::-1]:
        rows = pl.ds(pl.multiple_of(core * half + q * chunk + spot.flip(k) * piece, piece), piece)
        if k:
            settle(gw_any.at[rows], s["arsem"].at[q + k - 1])
        else:
            owns[q].wait()
        remote(gw_any.at[rows], gw_any.at[rows], s["ssem"].at[4], s["trsem"].at[0], 1)

    settle(s["fsend"], s["ssem"].at[0])
    settle(s["s0send"], s["ssem"].at[1])
    settle(s["s1recv"], s["ssem"].at[2])
    settle(s["s1recv"], s["ssem"].at[3])
    settle(s["gsend"], s["ssem"].at[5])
    for g, (lo, nb) in enumerate(upper):
        settle(s["xbuf"].at[g, :, pl.ds(0, (1 << nb) - 1)], s["ssem"].at[6 + g])
    settle(s["s0recv"], s["trsem"].at[0])
    settle(s["s0recv"], s["ssem"].at[4])


def finish(*refs):
    ins, outs, sem = refs[:3], refs[3:6], refs[6]
    copies = [pltpu.make_async_copy(a, b, sem.at[i]) for i, (a, b) in enumerate(zip(ins, outs))]
    for c in copies:
        c.start()
    for c in copies:
        c.wait()


def body(nbits, features, weight, grad_out, adjacency, tile_row, tile_src, tile_count,
         send_tile, stale_feat, stale_grad, blend):
    nodes, width = features.shape
    entries, block = adjacency.shape[:2]
    rounds = send_tile.shape[1]
    tiles = nodes // block
    scratch = names_and_shapes(tiles, block, width, entries, rounds, len(upper_stages(nbits)))
    hbm = pl.BlockSpec(memory_space=pltpu.HBM)
    free = pl.BlockSpec(memory_space=pl.ANY)
    results = (jax.ShapeDtypeStruct((nodes, width), BF16),
               jax.ShapeDtypeStruct((nodes, width), BF16),
               jax.ShapeDtypeStruct((width, width), BF16))
    found = pl.pallas_call(
        functools.partial(kernel, tuple(scratch), nbits),
        name="layer",
        out_shape=results,
        in_specs=[hbm] * 10 + [free],
        out_specs=(pl.BlockSpec(memory_space=pltpu.VMEM),) * 2 + (free,),
        scratch_shapes=list(scratch.values()),
        compiler_params=pltpu.CompilerParams(collective_id=0, has_side_effects=True,
                                             vmem_limit_bytes=48 * 1024 * 1024),
    )(*(pltpu.with_memory_space_constraint(x, pltpu.HBM) for x in (
        features.reshape(tiles, block, width), weight, grad_out, adjacency, stale_feat,
        stale_grad.reshape(rounds * block, width), blend.reshape(1, width),
        tile_row, tile_src, send_tile)), tile_count.reshape(1, 1))
    return tuple(pl.pallas_call(
        finish,
        name="finish",
        out_shape=results,
        in_specs=[free] * 3,
        out_specs=(hbm,) * 3,
        scratch_shapes=[pltpu.SemaphoreType.DMA((3,))],
        compiler_params=pltpu.CompilerParams(vmem_limit_bytes=16 * 1024 * 1024),
    )(*found))


def solution(mesh):
    nbits = mesh.shape["dom"].bit_length() - 1
    placed = (
        P("dom", None), P(), P("dom", None), P("dom", None, None), P("dom", None), P("dom", None),
        P("dom"), P("dom", None), P("dom", None, None, None), P("dom", None, None, None), P(),
    )
    return jax.shard_map(
        functools.partial(body, nbits),
        mesh=mesh,
        in_specs=placed,
        out_specs=(P("dom", None), P("dom", None), P()),
        check_vma=False,
    )
```

```python
import functools

import jax
import jax.numpy as jnp
from jax import lax
from jax.experimental import pallas as pl
from jax.experimental.pallas import tpu as pltpu
from jax.sharding import PartitionSpec as P

MESH = pl.DeviceIdType.MESH
F32 = jnp.float32
BF16 = jnp.bfloat16
CHUNKS = 2
GROUP_BITS = 3
GROUP = 1 << GROUP_BITS
NEAR_LAST = (7, 6, 5, 3, 4, 2, 1)


def bit_of(i, b):
    return lax.rem(lax.div(i, 1 << b), 2)


class Index:
    def __init__(self, value, bits):
        self.value = value
        self.step = [(1 - 2 * bit_of(value, b)) * (1 << b) for b in range(bits)]

    def flip(self, mask):
        out = self.value
        for b in range(mask.bit_length()):
            if mask >> b & 1:
                out = out + self.step[b]
        return out


def upper_stages(nbits):
    stages, b = [], 1 + GROUP_BITS
    while b < nbits:
        stages.append((b, min(2, nbits - b)))
        b += 2
    return stages


def names_and_shapes(tiles, block, width, entries, rounds, n_upper):
    nodes = tiles * block
    half = width // 2
    piece = half // CHUNKS // GROUP
    v = pltpu.VMEM
    return dict(
        feat=v((tiles, block, width), BF16),
        wgt=v((width, width), BF16),
        gout=v((nodes, width), BF16),
        adj=v((entries, block, block), BF16),
        sfeat=v((rounds, block, width), BF16),
        sgrad=v((rounds * block, width), BF16),
        fsend=v((rounds, block, width), BF16),
        frecv=v((rounds, block, width), BF16),
        used=v((rounds * block, width), BF16),
        chain=v((entries + 1, block, block), F32),
        dense=v((nodes, (tiles + rounds) * block), BF16),
        pick=v((nodes, rounds * block), BF16),
        edge=v((rounds * block, nodes), BF16),
        wgtt=v((width, width), BF16),
        part=v((nodes, width), F32),
        aggt=v((width, nodes), BF16),
        dpre=v((nodes, width), BF16),
        dagg=v((nodes, width), BF16),
        back=v((nodes, width), F32),
        gsend=v((rounds * block, width), BF16),
        grecv=v((rounds * block, width), BF16),
        s0send=v((half, width), BF16),
        s0recv=v((half, width), BF16),
        acc=v((half, width), F32),
        s1send=v((half, width), BF16),
        s1recv=v((CHUNKS, (GROUP - 1) * piece, width), BF16),
        xbuf=v((max(n_upper, 1), CHUNKS, 4, piece, width), BF16),
        mine=v((CHUNKS, piece, width), BF16),
        mixv=v((1, width), F32),
        row_s=pltpu.SMEM((1, entries), jnp.int32),
        src_s=pltpu.SMEM((1, entries), jnp.int32),
        tile_s=pltpu.SMEM((1, rounds), jnp.int32),
        count_s=pltpu.SMEM((1, 1), jnp.int32),
        lsem=pltpu.SemaphoreType.DMA((11,)),
        ssem=pltpu.SemaphoreType.DMA((6 + n_upper,)),
        frsem=pltpu.SemaphoreType.DMA((rounds,)),
        grsem=pltpu.SemaphoreType.DMA((1,)),
        crsem=pltpu.SemaphoreType.DMA((CHUNKS,)),
        rrsem=pltpu.SemaphoreType.DMA((CHUNKS,)),
        xrsem=pltpu.SemaphoreType.DMA((max(n_upper, 1) * CHUNKS,)),
        arsem=pltpu.SemaphoreType.DMA((CHUNKS - 1 + GROUP - 1,)),
        trsem=pltpu.SemaphoreType.DMA((1,)),
    )


def kernel(names, nbits, *refs):
    (features, weight, grad_out, adjacency, stale_feat, stale_grad, blend,
     row_hbm, src_hbm, tile_hbm, count_hbm, out_any, gf_any, gw_any) = refs[:14]
    s = dict(zip(names, refs[14:]))
    send_tile = s["tile_s"]
    tiles, block, width = s["feat"].shape
    rounds = s["fsend"].shape[0]
    entries = s["adj"].shape[0]
    nodes = tiles * block
    cells = tiles + rounds
    half = width // 2
    chunk = half // CHUNKS
    piece = chunk // GROUP
    me = Index(lax.axis_index("dom"), nbits)
    core = bit_of(me.value, 0)
    spot = Index(lax.rem(lax.div(me.value, 2), GROUP), GROUP_BITS)
    upper = upper_stages(nbits)

    def remote(src, dst, send, recv, mask):
        pltpu.make_async_remote_copy(
            src_ref=src, dst_ref=dst, send_sem=send, recv_sem=recv,
            device_id=(me.flip(mask),), device_id_type=MESH).start()

    def settle(ref, sem):
        pltpu.make_async_copy(ref, ref, sem).wait()

    round_mask = [1 << (r * nbits // rounds) for r in range(rounds)]
    peers = {1} | {k << 1 for k in range(1, GROUP)} | set(round_mask)
    for lo, nb in upper:
        peers |= {k << lo for k in range(1, 1 << nb)}
    barrier = pltpu.get_barrier_semaphore()
    for m in sorted(peers):
        pl.semaphore_signal(barrier, inc=1, device_id=(me.flip(m),), device_id_type=MESH)

    loads = {}
    for i, (src, name) in enumerate((
            (tile_hbm, "tile_s"), (features, "feat"), (row_hbm, "row_s"), (src_hbm, "src_s"),
            (count_hbm, "count_s"), (adjacency, "adj"), (blend, "mixv"), (stale_feat.at[0], "sfeat"),
            (weight, "wgt"), (grad_out, "gout"), (stale_grad, "sgrad"))):
        loads[name] = pltpu.make_async_copy(src, s[name], s["lsem"].at[i])
        loads[name].start()

    early = [0] + list(range(3, rounds))
    late = [r for r in range(rounds) if r not in early]
    place = {r: i for i, r in enumerate(early + late)}
    loads["tile_s"].wait()
    loads["feat"].wait()
    for r in late + early[::-1]:
        s["fsend"][r] = s["feat"][send_tile[0, r]]
    pl.semaphore_wait(barrier, len(peers))
    for r in late + early[::-1]:
        remote(s["fsend"].at[r], s["frecv"].at[r], s["ssem"].at[0], s["frsem"].at[r], round_mask[r])

    for name in ("row_s", "src_s", "count_s"):
        loads[name].wait()
    live = s["count_s"][0, 0]
    keys = [jnp.where(e < live, s["row_s"][0, e] * cells + s["src_s"][0, e], -1 - e) for e in range(entries)]
    loads["adj"].wait()
    s["chain"][0] = jnp.zeros((block, block), F32)
    for e in range(entries):
        prev = jnp.int32(0)
        for f in range(e):
            prev = jnp.where(keys[f] == keys[e], f + 1, prev)
        s["chain"][e + 1] = s["chain"][prev] + s["adj"][e].astype(F32)
    for t in range(tiles):
        for c in range(cells):
            last = jnp.int32(0)
            for e in range(entries):
                last = jnp.where(keys[e] == t * cells + c, e + 1, last)
            at = c if c < tiles else tiles + place[c - tiles]
            cell = s["chain"][last].astype(BF16)
            s["dense"][t * block:(t + 1) * block, at * block:(at + 1) * block] = cell
            if c >= tiles:
                s["edge"][(c - tiles) * block:(c - tiles + 1) * block, t * block:(t + 1) * block] = cell.T

    loads["mixv"].wait()
    mix = s["mixv"][...]
    keep = 1.0 - mix
    s["part"][...] = jnp.dot(s["dense"][:, :nodes], s["feat"][...].reshape(nodes, width),
                             preferred_element_type=F32)
    eye = (lax.broadcasted_iota(jnp.int32, (block, block), 0)
           == lax.broadcasted_iota(jnp.int32, (block, block), 1)).astype(F32)
    for t in range(tiles):
        for r in range(rounds):
            hot = jnp.where(send_tile[0, r] == t, 1.0, 0.0).astype(F32)
            s["pick"][t * block:(t + 1) * block, r * block:(r + 1) * block] = (eye * hot).astype(BF16)
    loads["sfeat"].wait()
    loads["wgt"].wait()
    s["wgtt"][...] = s["wgt"][...].T
    loads["gout"].wait()

    def blend_in(which):
        for r in which:
            pltpu.make_async_copy(s["frecv"].at[r], s["frecv"].at[r], s["frsem"].at[r]).wait()
            at = place[r]
            s["used"][at * block:(at + 1) * block, :] = (
                keep * s["sfeat"][r].astype(F32) + mix * s["frecv"][r].astype(F32)).astype(BF16)

    split = len(early) * block
    blend_in(early)
    s["part"][...] += jnp.dot(s["dense"][:, nodes:nodes + split], s["used"][:split, :],
                              preferred_element_type=F32)
    blend_in(late)
    step = 2 * block
    for t in range(nodes // step):
        rows = slice(t * step, (t + 1) * step)
        agg = (s["part"][rows, :] + jnp.dot(
            s["dense"][rows, nodes + split:], s["used"][split:, :],
            preferred_element_type=F32)).astype(BF16)
        s["aggt"][:, rows] = agg.T
        pre = jnp.dot(agg, s["wgt"][...], preferred_element_type=F32)
        sigma = jax.nn.sigmoid(pre)
        out = pre * sigma
        out_any[rows, :] = out.astype(BF16)
        s["dpre"][rows, :] = (s["gout"][rows, :].astype(F32) * sigma * (1.0 + pre * (1.0 - sigma))).astype(BF16)

    def chunk_product(h, q):
        return jnp.dot(s["aggt"][pl.ds(pl.multiple_of(h * half + q * chunk, chunk), chunk), :], s["dpre"][...],
                       preferred_element_type=F32)

    for q in range(CHUNKS):
        rows = pl.ds(q * chunk, chunk)
        s["s0send"][q * chunk:(q + 1) * chunk, :] = chunk_product(1 - core, q).astype(BF16)
        remote(s["s0send"].at[rows], s["s0recv"].at[rows], s["ssem"].at[1], s["crsem"].at[q], 1)
    for q in range(CHUNKS):
        s["acc"][q * chunk:(q + 1) * chunk, :] = chunk_product(core, q)

    def send_back(r):
        rows = pl.ds(r * block, block)
        remote(s["gsend"].at[rows], s["grecv"].at[rows], s["ssem"].at[5], s["grsem"].at[0], round_mask[r])

    def make_back():
        s["dagg"][...] = jnp.dot(s["dpre"][...], s["wgtt"][...], preferred_element_type=F32).astype(BF16)
        s["gsend"][...] = jnp.dot(s["edge"][...], s["dagg"][...], preferred_element_type=F32).astype(BF16)

    @pl.when(core == 1)
    def _():
        make_back()
        for r in late + early[::-1]:
            send_back(r)

    def own_rows(q, k=0):
        return pl.ds(pl.multiple_of(q * chunk + spot.flip(k) * piece, piece), piece)

    for q in range(CHUNKS):
        rows = slice(q * chunk, (q + 1) * chunk)
        settle(s["s0recv"].at[pl.ds(q * chunk, chunk)], s["crsem"].at[q])
        total = s["acc"][rows, :] + s["s0recv"][rows, :].astype(F32)
        s["acc"][rows, :] = total
        s["s1send"][rows, :] = total.astype(BF16)
        for k in NEAR_LAST:
            remote(s["s1send"].at[own_rows(q, k)], s["s1recv"].at[q, pl.ds((k - 1) * piece, piece)],
                   s["ssem"].at[2], s["rrsem"].at[q], k << 1)

    @pl.when(core == 0)
    def _():
        make_back()
        for r in early[:1]:
            send_back(r)

    loads["sgrad"].wait()
    s["back"][...] = lax.dot_general(s["dense"][:, :nodes], s["dagg"][...], (((0,), (0,)), ((), ())),
                                     preferred_element_type=F32) + keep * jnp.dot(
        s["pick"][...], s["sgrad"][...], preferred_element_type=F32)

    totals = []

    def swap(g, q, total):
        lo, nb = upper[g]
        at = lax.rem(lax.div(me.value, 1 << lo), 1 << nb)
        s["xbuf"][g, q, pl.ds(at, 1)] = total.astype(BF16)[None]
        for k in range(1, 1 << nb):
            remote(s["xbuf"].at[g, q, at], s["xbuf"].at[g, q, at], s["ssem"].at[6 + g],
                   s["xrsem"].at[g * CHUNKS + q], k << lo)

    def swapped(g, q):
        size = 1 << upper[g][1]
        settle(s["xbuf"].at[g, q, pl.ds(0, size - 1)], s["xrsem"].at[g * CHUNKS + q])
        total = s["xbuf"][g, q, 0].astype(F32)
        for x in range(1, size):
            total = total + s["xbuf"][g, q, x].astype(F32)
        return total

    def gw_rows(q):
        return pl.ds(pl.multiple_of(core * half + q * chunk + spot.value * piece, piece), piece)

    def spread(q, total):
        s["mine"][q] = total.astype(BF16)
        for k in NEAR_LAST:
            remote(s["mine"].at[q], gw_any.at[gw_rows(q)], s["ssem"].at[3],
                   s["arsem"].at[q if q < CHUNKS - 1 else q + k - 1], k << 1)
        own = pltpu.make_async_copy(s["mine"].at[q], gw_any.at[gw_rows(q)], s["lsem"].at[1 + q])
        own.start()
        return own

    owns = []
    for q in range(CHUNKS):
        settle(s["s1recv"].at[q], s["rrsem"].at[q])
        total = s["acc"][own_rows(q), :]
        for k in range(1, GROUP):
            total = total + s["s1recv"][q, (k - 1) * piece:k * piece, :].astype(F32)
        if upper:
            swap(0, q, total)
            if q == 0:
                @pl.when(core == 0)
                def _():
                    for r in late:
                        send_back(r)
        else:
            owns.append(spread(q, total))
    @pl.when(core == 0)
    def _():
        for r in early[:0:-1]:
            send_back(r)

    for g in range(len(upper)):
        for q in range(CHUNKS):
            total = swapped(g, q)
            if g + 1 < len(upper):
                swap(g + 1, q, total)
            else:
                owns.append(spread(q, total))

    settle(s["grecv"], s["grsem"].at[0])
    gf_any[...] = (s["back"][...] + mix * jnp.dot(
        s["pick"][...], s["grecv"][...], preferred_element_type=F32)).astype(BF16)

    for q in range(CHUNKS - 1):
        settle(s["s1recv"].at[q], s["arsem"].at[q])
        owns[q].wait()
        rows = pl.ds(pl.multiple_of(core * half + q * chunk, chunk), chunk)
        remote(gw_any.at[rows], gw_any.at[rows], s["ssem"].at[4], s["trsem"].at[0], 1)
    q = CHUNKS - 1
    for k in (0,) + NEAR_LAST[::-1]:
        rows = pl.ds(pl.multiple_of(core * half + q * chunk + spot.flip(k) * piece, piece), piece)
        if k:
            settle(gw_any.at[rows], s["arsem"].at[q + k - 1])
        else:
            owns[q].wait()
        remote(gw_any.at[rows], gw_any.at[rows], s["ssem"].at[4], s["trsem"].at[0], 1)

    settle(s["fsend"], s["ssem"].at[0])
    settle(s["s0send"], s["ssem"].at[1])
    settle(s["s1recv"], s["ssem"].at[2])
    settle(s["s1recv"], s["ssem"].at[3])
    settle(s["gsend"], s["ssem"].at[5])
    for g, (lo, nb) in enumerate(upper):
        settle(s["xbuf"].at[g, :, pl.ds(0, (1 << nb) - 1)], s["ssem"].at[6 + g])
    settle(s["s0recv"], s["trsem"].at[0])
    settle(s["s0recv"], s["ssem"].at[4])


def finish(*refs):
    ins, outs, sem = refs[:3], refs[3:6], refs[6]
    copies = [pltpu.make_async_copy(a, b, sem.at[i]) for i, (a, b) in enumerate(zip(ins, outs))]
    for c in copies:
        c.start()
    for c in copies:
        c.wait()


def body(nbits, features, weight, grad_out, adjacency, tile_row, tile_src, tile_count,
         send_tile, stale_feat, stale_grad, blend):
    nodes, width = features.shape
    entries, block = adjacency.shape[:2]
    rounds = send_tile.shape[1]
    tiles = nodes // block
    scratch = names_and_shapes(tiles, block, width, entries, rounds, len(upper_stages(nbits)))
    hbm = pl.BlockSpec(memory_space=pltpu.HBM)
    free = pl.BlockSpec(memory_space=pl.ANY)
    results = (jax.ShapeDtypeStruct((nodes, width), BF16),
               jax.ShapeDtypeStruct((nodes, width), BF16),
               jax.ShapeDtypeStruct((width, width), BF16))
    found = pl.pallas_call(
        functools.partial(kernel, tuple(scratch), nbits),
        name="layer",
        out_shape=results,
        in_specs=[hbm] * 10 + [free],
        out_specs=(pl.BlockSpec(memory_space=pltpu.VMEM),) * 2 + (free,),
        scratch_shapes=list(scratch.values()),
        compiler_params=pltpu.CompilerParams(collective_id=0, has_side_effects=True,
                                             vmem_limit_bytes=48 * 1024 * 1024),
    )(*(pltpu.with_memory_space_constraint(x, pltpu.HBM) for x in (
        features.reshape(tiles, block, width), weight, grad_out, adjacency, stale_feat,
        stale_grad.reshape(rounds * block, width), blend.reshape(1, width),
        tile_row, tile_src, send_tile)), tile_count.reshape(1, 1))
    return tuple(pl.pallas_call(
        finish,
        name="finish",
        out_shape=results,
        in_specs=[free] * 3,
        out_specs=(hbm,) * 3,
        scratch_shapes=[pltpu.SemaphoreType.DMA((3,))],
        compiler_params=pltpu.CompilerParams(vmem_limit_bytes=16 * 1024 * 1024),
    )(*found))


def solution(mesh):
    nbits = mesh.shape["dom"].bit_length() - 1
    placed = (
        P("dom", None), P(), P("dom", None), P("dom", None, None), P("dom", None), P("dom", None),
        P("dom"), P("dom", None), P("dom", None, None, None), P("dom", None, None, None), P(),
    )
    return jax.shard_map(
        functools.partial(body, nbits),
        mesh=mesh,
        in_specs=placed,
        out_specs=(P("dom", None), P("dom", None), P()),
        check_vma=False,
    )
```
